256 devices in a mesh: order: 16 (over y, x), level: 8 (over z), freq: 2 (over core).
Axes of the slice: x: 4, y: 4, z: 8, core: 2. Of those that a mesh axis runs over, the one named last changes fastest.
Arguments:
- fourier: bfloat16 [64, 8, 8, 128, 512], P('freq', None, 'level', 'order'), parts along dimension 0, may hold values from -6 to 6
- order_slot: int32 [32], replicated, may hold values from 0 to 31, each once
- coeff_self: bfloat16 [6, 32, 64, 128, 128], P(None, 'order', 'level'), may hold values from -0.375 to 0.375
- coeff_pair: bfloat16 [6, 32, 64, 128, 128], P(None, 'order', 'level'), may hold values from -0.375 to 0.375
Outputs:
- butterfly: bfloat16 [64, 64, 128, 512], P(('freq', 'order'), 'level'), parts along dimension 0
The draws below stay inside these ranges and needn't reach their ends.
There are 2 independent parts, one for each index of `freq`. The reference program is written for one: setup_inputs(seed, part) draws one part's arguments, and reference() takes and returns one part's arrays. A program takes and returns all parts, laid end to end along the dimension named above; an argument that names none is the same for every part. Nothing has to cross between parts.
Inputs may be any that keep to these rules, and one draw needn't show every extreme that they name: order_slot is a permutation of the orders.
All inputs are finite; a program needn't handle non-finite values.
Results may differ from the reference program's by a relative error of at most 0.008.
Values may be sent and summed in bfloat16 or wider, within the bound.
A program may use at most 64 MiB of HBM per device.

```python
import jax
import jax.numpy as jnp

ROWS = 128
FIELDS = 256
LEAVES = 64
LEVELS = 6
BLK_DEV = 8
ORDERS = 32
N_LEVEL = 8


def level_of(key, shape, shards, low, top_value):
    def one(axis_at, blocks):
        draws = jax.random.uniform(jax.random.fold_in(jax.random.fold_in(key, 6), axis_at), (blocks,), jnp.float32, low / len(shards), top_value / len(shards))
        return jnp.repeat(jnp.exp(draws), shape[axis_at] // blocks).reshape((-1,) + (1,) * (len(shape) - axis_at - 1))

    level = one(*shards[0])
    for cut in shards[1:]:
        level = level * one(*cut)
    return level


def noise(stream_key, dims, spread, bound, cuts=(), kind=jnp.bfloat16):
    drawn = spread * jax.random.normal(stream_key, dims, jnp.float32)
    if cuts:
        drawn = drawn * level_of(stream_key, dims, cuts, -0.22, 0.18)
    return jnp.clip(drawn, -bound, bound).astype(kind)


def setup_inputs(seed: int = 0, part: int = 0) -> dict:
    arg_keys = jax.random.split(jax.random.key(seed), 5)
    own_keys = jax.random.split(jax.random.fold_in(arg_keys[4], part), 5)
    return {
        "fourier": noise(own_keys[0], (ORDERS, BLK_DEV, N_LEVEL, ROWS, 2 * FIELDS), 1.0, 6.0, ((2, 8), (3, 16))),
        "order_slot": jax.random.permutation(arg_keys[1], ORDERS).astype(jnp.int32),
        "coeff_self": noise(arg_keys[2], (LEVELS, ORDERS, LEAVES, ROWS, ROWS), (2 * ROWS) ** -0.5, 0.375, ((1, 16), (2, 8))),
        "coeff_pair": noise(arg_keys[3], (LEVELS, ORDERS, LEAVES, ROWS, ROWS), (2 * ROWS) ** -0.5, 0.375, ((1, 16), (2, 8))),
    }


def partner_blocks(values, height):
    extent = values.shape
    halves = values.reshape(extent[0], extent[1] >> (height + 1), 2, 1 << height, extent[2], extent[3])
    return halves[:, :, ::-1].reshape(extent)


def reference(fourier, order_slot, coeff_self, coeff_pair):
    current = jnp.take(fourier, order_slot.astype(jnp.int32), axis=0)
    current = current.reshape(ORDERS, LEAVES, ROWS, 2 * FIELDS)
    for height in range(LEVELS):
        partner = partner_blocks(current, height)
        mixed_sum = jnp.einsum("sbrq,sbqc->sbrc", coeff_self[height].astype(jnp.float32), current.astype(jnp.float32))
        mixed_sum = mixed_sum + jnp.einsum("sbrq,sbqc->sbrc", coeff_pair[height].astype(jnp.float32), partner.astype(jnp.float32))
        current = mixed_sum.astype(jnp.bfloat16)
    return current
```

```python
import functools

import jax
import jax.numpy as jnp
from jax import lax
from jax.experimental import pallas as pl
from jax.experimental.pallas import tpu as pltpu
from jax.sharding import PartitionSpec as P

MESH = pl.DeviceIdType.MESH
CHUNKS = 2


def mix(buf, c, coef, levels, slots, blocks):
    half = blocks // 2
    for k in range(levels):
        step = 1 << k

        def pair(i, carry, k=k, step=step):
            slot = lax.div(i, half)
            p = lax.rem(i, half)
            low = lax.div(p, step) * (2 * step) + lax.rem(p, step)
            high = low + step
            both = jnp.concatenate([buf[c, low, slot], buf[c, high, slot]], axis=0)
            top = jnp.concatenate([coef[0, k, slot, low], coef[1, k, slot, low]], axis=1)
            bottom = jnp.concatenate([coef[1, k, slot, high], coef[0, k, slot, high]], axis=1)
            rows = top.shape[0]
            mixed = jnp.dot(
                jnp.concatenate([top, bottom], axis=0), both, preferred_element_type=jnp.float32
            ).astype(jnp.bfloat16)
            buf[c, low, slot] = mixed[:rows]
            buf[c, high, slot] = mixed[rows:]
            return carry

        lax.fori_loop(0, slots * half, pair, 0)


def kernel(
    n_order, n_level, slot_ref, fourier_ref, self_ref, pair_ref, out_ref,
    cycles, stage, by_cycle, blocks, turned, near, far,
    load_sem, own_sem, z1_sem, xy_sem, z2_sem, z3_sem, coef_sem, core_sem,
):
    o, z, f = lax.axis_index("order"), lax.axis_index("level"), lax.axis_index("freq")
    chunks = stage.shape[0]
    orders, rows, width = stage.shape[2:]
    slots = orders // n_order
    levels = near.shape[1]
    other = 1 - f

    def at_level(d):
        return lax.rem(z + d, n_level)

    def at_order(d):
        return lax.rem(o + d, n_order)

    def loop(count, body):
        lax.fori_loop(1, count, lambda d, carry: (body(d), carry)[1], 0)

    loads = [
        pltpu.make_async_copy(fourier_ref, cycles, load_sem.at[0]),
        pltpu.make_async_copy(self_ref.at[pl.ds(0, levels)], near.at[0], load_sem.at[1]),
        pltpu.make_async_copy(pair_ref.at[pl.ds(0, levels)], near.at[1], load_sem.at[2]),
        pltpu.make_async_copy(self_ref.at[pl.ds(levels, levels), f, z], far.at[0, :, f, z], load_sem.at[3]),
        pltpu.make_async_copy(pair_ref.at[pl.ds(levels, levels), f, z], far.at[1, :, f, z], load_sem.at[4]),
    ]
    for copy in loads:
        copy.start()

    barrier = pltpu.get_barrier_semaphore()
    loop(n_level, lambda d: pl.semaphore_signal(barrier, 1, device_id=(o, at_level(d), f), device_id_type=MESH))
    loop(n_order, lambda d: pl.semaphore_signal(barrier, 1, device_id=(at_order(d), z, f), device_id_type=MESH))
    pl.semaphore_signal(barrier, 1, device_id=(o, z, other), device_id_type=MESH)
    pl.semaphore_wait(barrier, n_level + n_order - 1)

    def to_level(src, dst, sems, c, d):
        return pltpu.make_async_remote_copy(
            src, dst, sems.at[0, c, d], sems.at[1, c, d],
            device_id=(o, at_level(d), f), device_id_type=MESH,
        )

    def z1(c, d):
        return to_level(stage.at[c, at_level(d)], by_cycle.at[c, z], z1_sem, c, d)

    def xy(c, d):
        return pltpu.make_async_remote_copy(
            by_cycle.at[c, :, pl.ds(at_order(d) * slots, slots)],
            blocks.at[c, :, :, pl.ds(pl.multiple_of(o * rows, rows), rows)],
            xy_sem.at[0, c, d], xy_sem.at[1, c, d],
            device_id=(at_order(d), z, f), device_id_type=MESH,
        )

    def z2(c, d):
        return to_level(blocks.at[c, at_level(d)], turned.at[c, z], z2_sem, c, d)

    def z3(c, d):
        return to_level(
            turned.at[c, at_level(d)], out_ref.at[:, z, :, pl.ds(c * width, width)], z3_sem, c, d
        )

    def coef(which, d):
        src = (self_ref, pair_ref)[which]
        return to_level(
            src.at[pl.ds(levels, levels), f, at_level(d)], far.at[which, :, f, z], coef_sem, which, d
        )

    def core(which):
        return pltpu.make_async_remote_copy(
            far.at[which, :, f], far.at[which, :, f],
            core_sem.at[0, which], core_sem.at[1, which],
            device_id=(o, z, other), device_id_type=MESH,
        )

    own = {}
    for c in range(chunks):
        own["xy", c] = pltpu.make_async_copy(
            by_cycle.at[c, :, pl.ds(o * slots, slots)],
            blocks.at[c, :, :, pl.ds(pl.multiple_of(o * rows, rows), rows)],
            own_sem.at[0, c],
        )
        own["z2", c] = pltpu.make_async_copy(blocks.at[c, z], turned.at[c, z], own_sem.at[1, c])
        own["z3", c] = pltpu.make_async_copy(
            turned.at[c, z], out_ref.at[:, z, :, pl.ds(c * width, width)], own_sem.at[2, c]
        )

    loads[0].wait()
    for c in range(chunks):

        def place(s, carry, c=c):
            order = slot_ref[s]
            stage[c, :, s] = cycles[order, :, :, c * width : (c + 1) * width]
            by_cycle[c, z, s] = cycles[order, z, :, c * width : (c + 1) * width]
            return carry

        lax.fori_loop(0, orders, place, 0)
        loop(n_level, lambda d: z1(c, d).start())
    for which in range(2):
        loop(n_level, lambda d: coef(which, d).start())

    for copy in loads[1:]:
        copy.wait()
    for c in range(chunks):
        loop(n_level, lambda d: z1(c, d).wait_recv())
        loop(n_order, lambda d: xy(c, d).start())
        own["xy", c].start()
        own["xy", c].wait()
        loop(n_order, lambda d: xy(c, d).wait_recv())
        mix(blocks, c, near, levels, slots, n_level)
        loop(n_level, lambda d: z2(c, d).start())
        own["z2", c].start()

    for which in range(2):
        loop(n_level, lambda d: coef(which, d).wait_recv())
        core(which).start()
    for which in range(2):
        core(which).wait_recv()

    for c in range(chunks):
        own["z2", c].wait()
        loop(n_level, lambda d: z2(c, d).wait_recv())
        mix(turned, c, far, levels, slots, n_level)
        loop(n_level, lambda d: z3(c, d).start())
        own["z3", c].start()

    for which in range(2):
        loop(n_level, lambda d: coef(which, d).wait_send())
        core(which).wait_send()
    for c in range(chunks):
        loop(n_level, lambda d: z1(c, d).wait_send())
        loop(n_order, lambda d: xy(c, d).wait_send())
        loop(n_level, lambda d: z2(c, d).wait_send())
        own["z3", c].wait()
        loop(n_level, lambda d: z3(c, d).wait())


def local(n_order, n_level, fourier, order_slot, coeff_self, coeff_pair):
    orders, groups, _, rows, columns = fourier.shape
    all_levels, slots, blocks, cycle_rows, _ = coeff_self.shape
    levels = all_levels // 2
    width = columns // CHUNKS
    dtype = jnp.bfloat16
    hbm = pl.BlockSpec(memory_space=pl.ANY)
    coefs = pltpu.VMEM((2, levels, slots, blocks, cycle_rows, cycle_rows), dtype)
    spread = pltpu.VMEM((CHUNKS, n_level, orders, rows, width), dtype)
    whole = pltpu.VMEM((CHUNKS, n_level, slots, cycle_rows, width), dtype)
    dma = pltpu.SemaphoreType.DMA
    return pl.pallas_call(
        functools.partial(kernel, n_order, n_level),
        out_shape=jax.ShapeDtypeStruct((slots, blocks, cycle_rows, columns), dtype),
        in_specs=[pl.BlockSpec(memory_space=pltpu.SMEM), hbm, hbm, hbm],
        out_specs=hbm,
        scratch_shapes=[
            pltpu.VMEM((orders, groups, rows, columns), dtype),
            spread, spread, whole, whole, coefs, coefs,
            dma((5,)), dma((3, CHUNKS)),
            dma((2, CHUNKS, n_level)), dma((2, CHUNKS, n_order)),
            dma((2, CHUNKS, n_level)), dma((2, CHUNKS, n_level)),
            dma((2, 2, n_level)), dma((2, 2)),
        ],
        compiler_params=pltpu.CompilerParams(
            collective_id=0, has_side_effects=True, vmem_limit_bytes=40 << 20
        ),
        name="butterfly",
    )(order_slot, fourier.reshape(orders, groups, rows, columns), coeff_self, coeff_pair)


def solution(mesh):
    placed = (
        P("freq", None, "level", "order", None),
        P(),
        P(None, "order", "level", None, None),
        P(None, "order", "level", None, None),
    )
    return jax.shard_map(
        functools.partial(local, mesh.shape["order"], mesh.shape["level"]),
        mesh=mesh,
        in_specs=placed,
        out_specs=P(("freq", "order"), "level", None, None),
        check_vma=False,
    )
```

```python
import functools

import jax
import jax.numpy as jnp
from jax import lax
from jax.experimental import pallas as pl
from jax.experimental.pallas import tpu as pltpu
from jax.sharding import PartitionSpec as P

MESH = pl.DeviceIdType.MESH
CHUNKS = 2


def mix(buf, c, coef, levels, slots, blocks):
    half = blocks // 2
    for k in range(levels):
        step = 1 << k

        def pair(i, carry, k=k, step=step):
            slot = lax.div(i, half)
            p = lax.rem(i, half)
            low = lax.div(p, step) * (2 * step) + lax.rem(p, step)
            high = low + step
            both = jnp.concatenate([buf[c, low, slot], buf[c, high, slot]], axis=0)
            top = jnp.concatenate([coef[0, k, slot, low], coef[1, k, slot, low]], axis=1)
            bottom = jnp.concatenate([coef[1, k, slot, high], coef[0, k, slot, high]], axis=1)
            rows = top.shape[0]
            mixed = jnp.dot(
                jnp.concatenate([top, bottom], axis=0), both, preferred_element_type=jnp.float32
            ).astype(jnp.bfloat16)
            buf[c, low, slot] = mixed[:rows]
            buf[c, high, slot] = mixed[rows:]
            return carry

        lax.fori_loop(0, slots * half, pair, 0)


def kernel(
    n_order, n_level, slot_ref, fourier_ref, self_ref, pair_ref, out_ref,
    cycles, stage, by_cycle, blocks, turned, near, far,
    load_sem, own_sem, z1_sem, xy_sem, z2_sem, z3_sem, coef_sem, core_sem,
):
    o, z, f = lax.axis_index("order"), lax.axis_index("level"), lax.axis_index("freq")
    chunks = stage.shape[0]
    orders, rows, width = stage.shape[2:]
    slots = orders // n_order
    levels = near.shape[1]
    other = 1 - f

    def at_level(d):
        return lax.rem(z + d, n_level)

    def at_order(d):
        return lax.rem(o + d, n_order)

    def loop(count, body):
        lax.fori_loop(1, count, lambda d, carry: (body(d), carry)[1], 0)

    loads = [
        pltpu.make_async_copy(fourier_ref, cycles, load_sem.at[0]),
        pltpu.make_async_copy(self_ref.at[pl.ds(0, levels)], near.at[0], load_sem.at[1]),
        pltpu.make_async_copy(pair_ref.at[pl.ds(0, levels)], near.at[1], load_sem.at[2]),
        pltpu.make_async_copy(self_ref.at[pl.ds(levels, levels), f, z], far.at[0, :, f, z], load_sem.at[3]),
        pltpu.make_async_copy(pair_ref.at[pl.ds(levels, levels), f, z], far.at[1, :, f, z], load_sem.at[4]),
    ]
    for copy in loads:
        copy.start()

    barrier = pltpu.get_barrier_semaphore()
    loop(n_level, lambda d: pl.semaphore_signal(barrier, 1, device_id=(o, at_level(d), f), device_id_type=MESH))
    loop(n_order, lambda d: pl.semaphore_signal(barrier, 1, device_id=(at_order(d), z, f), device_id_type=MESH))
    pl.semaphore_signal(barrier, 1, device_id=(o, z, other), device_id_type=MESH)
    pl.semaphore_wait(barrier, n_level + n_order - 1)

    def to_level(src, dst, sems, c, d):
        return pltpu.make_async_remote_copy(
            src, dst, sems.at[0, c, d], sems.at[1, c, d],
            device_id=(o, at_level(d), f), device_id_type=MESH,
        )

    def z1(c, d):
        return to_level(stage.at[c, at_level(d)], by_cycle.at[c, z], z1_sem, c, d)

    def xy(c, d):
        return pltpu.make_async_remote_copy(
            by_cycle.at[c, :, pl.ds(at_order(d) * slots, slots)],
            blocks.at[c, :, :, pl.ds(pl.multiple_of(o * rows, rows), rows)],
            xy_sem.at[0, c, d], xy_sem.at[1, c, d],
            device_id=(at_order(d), z, f), device_id_type=MESH,
        )

    def z2(c, d):
        return to_level(blocks.at[c, at_level(d)], turned.at[c, z], z2_sem, c, d)

    def z3(c, d):
        return to_level(
            turned.at[c, at_level(d)], out_ref.at[:, z, :, pl.ds(c * width, width)], z3_sem, c, d
        )

    def coef(which, d):
        src = (self_ref, pair_ref)[which]
        return to_level(
            src.at[pl.ds(levels, levels), f, at_level(d)], far.at[which, :, f, z], coef_sem, which, d
        )

    def core(which):
        return pltpu.make_async_remote_copy(
            far.at[which, :, f], far.at[which, :, f],
            core_sem.at[0, which], core_sem.at[1, which],
            device_id=(o, z, other), device_id_type=MESH,
        )

    own = {}
    for c in range(chunks):
        own["xy", c] = pltpu.make_async_copy(
            by_cycle.at[c, :, pl.ds(o * slots, slots)],
            blocks.at[c, :, :, pl.ds(pl.multiple_of(o * rows, rows), rows)],
            own_sem.at[0, c],
        )
        own["z2", c] = pltpu.make_async_copy(blocks.at[c, z], turned.at[c, z], own_sem.at[1, c])
        own["z3", c] = pltpu.make_async_copy(
            turned.at[c, z], out_ref.at[:, z, :, pl.ds(c * width, width)], own_sem.at[2, c]
        )

    loads[0].wait()
    for c in range(chunks):

        def place(s, carry, c=c):
            order = slot_ref[s]
            stage[c, :, s] = cycles[order, :, :, c * width : (c + 1) * width]
            by_cycle[c, z, s] = cycles[order, z, :, c * width : (c + 1) * width]
            return carry

        lax.fori_loop(0, orders, place, 0)
        loop(n_level, lambda d: z1(c, d).start())
    for which in range(2):
        loop(n_level, lambda d: coef(which, d).start())

    for copy in loads[1:]:
        copy.wait()
    for c in range(chunks):
        loop(n_level, lambda d: z1(c, d).wait_recv())
        loop(n_order, lambda d: xy(c, d).start())
        own["xy", c].start()
        own["xy", c].wait()
        loop(n_order, lambda d: xy(c, d).wait_recv())
        mix(blocks, c, near, levels, slots, n_level)
        loop(n_level, lambda d: z2(c, d).start())
        own["z2", c].start()

    for which in range(2):
        loop(n_level, lambda d: coef(which, d).wait_recv())
        core(which).start()
    for which in range(2):
        core(which).wait_recv()

    for c in range(chunks):
        own["z2", c].wait()
        loop(n_level, lambda d: z2(c, d).wait_recv())
        mix(turned, c, far, levels, slots, n_level)
        loop(n_level, lambda d: z3(c, d).start())
        own["z3", c].start()

    for which in range(2):
        loop(n_level, lambda d: coef(which, d).wait_send())
        core(which).wait_send()
    for c in range(chunks):
        loop(n_level, lambda d: z1(c, d).wait_send())
        loop(n_order, lambda d: xy(c, d).wait_send())
        loop(n_level, lambda d: z2(c, d).wait_send())
        own["z3", c].wait()
        loop(n_level, lambda d: z3(c, d).wait())


def local(n_order, n_level, fourier, order_slot, coeff_self, coeff_pair):
    orders, groups, _, rows, columns = fourier.shape
    all_levels, slots, blocks, cycle_rows, _ = coeff_self.shape
    levels = all_levels // 2
    width = columns // CHUNKS
    dtype = jnp.bfloat16
    hbm = pl.BlockSpec(memory_space=pl.ANY)
    coefs = pltpu.VMEM((2, levels, slots, blocks, cycle_rows, cycle_rows), dtype)
    spread = pltpu.VMEM((CHUNKS, n_level, orders, rows, width), dtype)
    whole = pltpu.VMEM((CHUNKS, n_level, slots, cycle_rows, width), dtype)
    dma = pltpu.SemaphoreType.DMA
    return pl.pallas_call(
        functools.partial(kernel, n_order, n_level),
        out_shape=jax.ShapeDtypeStruct((slots, blocks, cycle_rows, columns), dtype),
        in_specs=[pl.BlockSpec(memory_space=pltpu.SMEM), hbm, hbm, hbm],
        out_specs=hbm,
        scratch_shapes=[
            pltpu.VMEM((orders, groups, rows, columns), dtype),
            spread, spread, whole, whole, coefs, coefs,
            dma((5,)), dma((3, CHUNKS)),
            dma((2, CHUNKS, n_level)), dma((2, CHUNKS, n_order)),
            dma((2, CHUNKS, n_level)), dma((2, CHUNKS, n_level)),
            dma((2, 2, n_level)), dma((2, 2)),
        ],
        compiler_params=pltpu.CompilerParams(
            collective_id=0, has_side_effects=True, vmem_limit_bytes=50 << 20
        ),
        name="butterfly",
    )(order_slot, fourier.reshape(orders, groups, rows, columns), coeff_self, coeff_pair)


def solution(mesh):
    placed = (
        P("freq", None, "level", "order", None),
        P(),
        P(None, "order", "level", None, None),
        P(None, "order", "level", None, None),
    )
    return jax.shard_map(
        functools.partial(local, mesh.shape["order"], mesh.shape["level"]),
        mesh=mesh,
        in_specs=placed,
        out_specs=P(("freq", "order"), "level", None, None),
        check_vma=False,
    )
```

```python
import functools

import jax
import jax.numpy as jnp
from jax import lax
from jax.experimental import pallas as pl
from jax.experimental.pallas import tpu as pltpu
from jax.sharding import PartitionSpec as P

MESH = pl.DeviceIdType.MESH
CHUNKS = 2
LEADER = 0
HERALD = 1


def mix(buf, c, coef, levels, slots, blocks):
    half = blocks // 2
    for k in range(levels):
        step = 1 << k

        def pair(i, carry, k=k, step=step):
            slot = lax.div(i, half)
            p = lax.rem(i, half)
            low = lax.div(p, step) * (2 * step) + lax.rem(p, step)
            high = low + step
            both = jnp.concatenate([buf[c, low, slot], buf[c, high, slot]], axis=0)
            top = jnp.concatenate([coef[0, k, slot, low], coef[1, k, slot, low]], axis=1)
            bottom = jnp.concatenate([coef[1, k, slot, high], coef[0, k, slot, high]], axis=1)
            rows = top.shape[0]
            mixed = jnp.dot(
                jnp.concatenate([top, bottom], axis=0), both, preferred_element_type=jnp.float32
            ).astype(jnp.bfloat16)
            buf[c, low, slot] = mixed[:rows]
            buf[c, high, slot] = mixed[rows:]
            return carry

        lax.fori_loop(0, slots * half, pair, 0)


def kernel(
    n_order, n_level, slot_ref, fourier_ref, self_ref, pair_ref, out_ref,
    cycles, stage, by_cycle, blocks, turned, near, far,
    joined, opened, load_sem, own_sem, z1_sem, xy_sem, z2_sem, z3_sem, coef_sem, core_sem,
):
    o, z, f = lax.axis_index("order"), lax.axis_index("level"), lax.axis_index("freq")
    chunks = stage.shape[0]
    orders, rows, width = stage.shape[2:]
    slots = orders // n_order
    levels = near.shape[1]
    other = 1 - f

    def at_level(d):
        return lax.rem(z + d, n_level)

    def at_order(d):
        return lax.rem(o + d, n_order)

    def loop(count, body):
        lax.fori_loop(1, count, lambda d, carry: (body(d), carry)[1], 0)

    loads = [
        pltpu.make_async_copy(fourier_ref, cycles, load_sem.at[0]),
        pltpu.make_async_copy(self_ref.at[pl.ds(0, levels)], near.at[0], load_sem.at[1]),
        pltpu.make_async_copy(pair_ref.at[pl.ds(0, levels)], near.at[1], load_sem.at[2]),
        pltpu.make_async_copy(self_ref.at[pl.ds(levels, levels), f, z], far.at[0, :, f, z], load_sem.at[3]),
        pltpu.make_async_copy(pair_ref.at[pl.ds(levels, levels), f, z], far.at[1, :, f, z], load_sem.at[4]),
    ]
    for copy in loads:
        copy.start()

    barrier = pltpu.get_barrier_semaphore()

    def greet(d):
        @pl.when(at_level(d) != LEADER)
        def _():
            pl.semaphore_signal(barrier, 1, device_id=(o, at_level(d), f), device_id_type=MESH)

    loop(n_level, greet)
    pl.semaphore_signal(barrier, 1, device_id=(o, z, other), device_id_type=MESH)

    def enter():
        @pl.when(z != LEADER)
        def _():
            pl.semaphore_wait(barrier, n_level)
            pl.semaphore_signal(joined, 1, device_id=(o, LEADER, f), device_id_type=MESH)

        @pl.when(z == LEADER)
        def _():
            pl.semaphore_wait(joined, n_level - 1)

    def herald():
        @pl.when(z == HERALD)
        def _():
            loop(n_order, lambda d: pl.semaphore_signal(
                barrier, 1, device_id=(at_order(d), LEADER, f), device_id_type=MESH
            ))

    def meet_columns():
        @pl.when(z == LEADER)
        def _():
            pl.semaphore_wait(barrier, n_order)
            loop(n_level, lambda d: pl.semaphore_signal(
                opened, 1, device_id=(o, at_level(d), f), device_id_type=MESH
            ))

        @pl.when(z != LEADER)
        def _():
            pl.semaphore_wait(opened, 1)

    def to_level(src, dst, sems, c, d):
        return pltpu.make_async_remote_copy(
            src, dst, sems.at[0, c, d], sems.at[1, c, d],
            device_id=(o, at_level(d), f), device_id_type=MESH,
        )

    def z1(c, d):
        return to_level(stage.at[c, at_level(d)], by_cycle.at[c, z], z1_sem, c, d)

    def xy(c, d):
        return pltpu.make_async_remote_copy(
            by_cycle.at[c, :, pl.ds(at_order(d) * slots, slots)],
            blocks.at[c, :, :, pl.ds(pl.multiple_of(o * rows, rows), rows)],
            xy_sem.at[0, c, d], xy_sem.at[1, c, d],
            device_id=(at_order(d), z, f), device_id_type=MESH,
        )

    def z2(c, d):
        return to_level(blocks.at[c, at_level(d)], turned.at[c, z], z2_sem, c, d)

    def z3(c, d):
        return to_level(
            turned.at[c, at_level(d)], out_ref.at[:, z, :, pl.ds(c * width, width)], z3_sem, c, d
        )

    def coef(which, d):
        src = (self_ref, pair_ref)[which]
        return to_level(
            src.at[pl.ds(levels, levels), f, at_level(d)], far.at[which, :, f, z], coef_sem, which, d
        )

    def core(which):
        return pltpu.make_async_remote_copy(
            far.at[which, :, f], far.at[which, :, f],
            core_sem.at[0, which], core_sem.at[1, which],
            device_id=(o, z, other), device_id_type=MESH,
        )

    own = {}
    for c in range(chunks):
        own["xy", c] = pltpu.make_async_copy(
            by_cycle.at[c, :, pl.ds(o * slots, slots)],
            blocks.at[c, :, :, pl.ds(pl.multiple_of(o * rows, rows), rows)],
            own_sem.at[0, c],
        )
        own["z2", c] = pltpu.make_async_copy(blocks.at[c, z], turned.at[c, z], own_sem.at[1, c])
        own["z3", c] = pltpu.make_async_copy(
            turned.at[c, z], out_ref.at[:, z, :, pl.ds(c * width, width)], own_sem.at[2, c]
        )

    loads[0].wait()
    for c in range(chunks):

        def place(s, carry, c=c):
            order = slot_ref[s]
            stage[c, :, s] = cycles[order, :, :, c * width : (c + 1) * width]
            by_cycle[c, z, s] = cycles[order, z, :, c * width : (c + 1) * width]
            return carry

        lax.fori_loop(0, orders, place, 0)
        if c == 0:
            enter()
        loop(n_level, lambda d: z1(c, d).start())
        if c == 0:
            herald()
    for which in range(2):
        loop(n_level, lambda d: coef(which, d).start())

    for copy in loads[1:]:
        copy.wait()
    for c in range(chunks):
        loop(n_level, lambda d: z1(c, d).wait_recv())
        if c == 0:
            meet_columns()
        loop(n_order, lambda d: xy(c, d).start())
        own["xy", c].start()
        own["xy", c].wait()
        loop(n_order, lambda d: xy(c, d).wait_recv())
        mix(blocks, c, near, levels, slots, n_level)
        loop(n_level, lambda d: z2(c, d).start())
        own["z2", c].start()

    for which in range(2):
        loop(n_level, lambda d: coef(which, d).wait_recv())
        core(which).start()
    for which in range(2):
        core(which).wait_recv()

    for c in range(chunks):
        own["z2", c].wait()
        loop(n_level, lambda d: z2(c, d).wait_recv())
        mix(turned, c, far, levels, slots, n_level)
        loop(n_level, lambda d: z3(c, d).start())
        own["z3", c].start()

    for which in range(2):
        loop(n_level, lambda d: coef(which, d).wait_send())
        core(which).wait_send()
    for c in range(chunks):
        loop(n_level, lambda d: z1(c, d).wait_send())
        loop(n_order, lambda d: xy(c, d).wait_send())
        loop(n_level, lambda d: z2(c, d).wait_send())
        own["z3", c].wait()
        loop(n_level, lambda d: z3(c, d).wait())


def local(n_order, n_level, fourier, order_slot, coeff_self, coeff_pair):
    orders, groups, _, rows, columns = fourier.shape
    all_levels, slots, blocks, cycle_rows, _ = coeff_self.shape
    levels = all_levels // 2
    width = columns // CHUNKS
    dtype = jnp.bfloat16
    hbm = pl.BlockSpec(memory_space=pl.ANY)
    coefs = pltpu.VMEM((2, levels, slots, blocks, cycle_rows, cycle_rows), dtype)
    spread = pltpu.VMEM((CHUNKS, n_level, orders, rows, width), dtype)
    whole = pltpu.VMEM((CHUNKS, n_level, slots, cycle_rows, width), dtype)
    dma = pltpu.SemaphoreType.DMA
    return pl.pallas_call(
        functools.partial(kernel, n_order, n_level),
        out_shape=jax.ShapeDtypeStruct((slots, blocks, cycle_rows, columns), dtype),
        in_specs=[pl.BlockSpec(memory_space=pltpu.SMEM), hbm, hbm, hbm],
        out_specs=hbm,
        scratch_shapes=[
            pltpu.VMEM((orders, groups, rows, columns), dtype),
            spread, spread, whole, whole, coefs, coefs,
            pltpu.SemaphoreType.REGULAR, pltpu.SemaphoreType.REGULAR,
            dma((5,)), dma((3, CHUNKS)),
            dma((2, CHUNKS, n_level)), dma((2, CHUNKS, n_order)),
            dma((2, CHUNKS, n_level)), dma((2, CHUNKS, n_level)),
            dma((2, 2, n_level)), dma((2, 2)),
        ],
        compiler_params=pltpu.CompilerParams(
            collective_id=0, has_side_effects=True, vmem_limit_bytes=50 << 20
        ),
        name="butterfly",
    )(order_slot, fourier.reshape(orders, groups, rows, columns), coeff_self, coeff_pair)


def solution(mesh):
    placed = (
        P("freq", None, "level", "order", None),
        P(),
        P(None, "order", "level", None, None),
        P(None, "order", "level", None, None),
    )
    return jax.shard_map(
        functools.partial(local, mesh.shape["order"], mesh.shape["level"]),
        mesh=mesh,
        in_specs=placed,
        out_specs=P(("freq", "order"), "level", None, None),
        check_vma=False,
    )
```

```python
import functools

import jax
import jax.numpy as jnp
from jax import lax
from jax.experimental import pallas as pl
from jax.experimental.pallas import tpu as pltpu
from jax.sharding import PartitionSpec as P

MESH = pl.DeviceIdType.MESH
CHUNKS = 2
LEADER = 2
HERALD = 1


def mix(buf, c, coef, levels, slots, blocks):
    half = blocks // 2
    for k in range(levels):
        step = 1 << k

        def pair(i, carry, k=k, step=step):
            slot = lax.div(i, half)
            p = lax.rem(i, half)
            low = lax.div(p, step) * (2 * step) + lax.rem(p, step)
            high = low + step
            both = jnp.concatenate([buf[c, low, slot], buf[c, high, slot]], axis=0)
            top = jnp.concatenate([coef[0, k, slot, low], coef[1, k, slot, low]], axis=1)
            bottom = jnp.concatenate([coef[1, k, slot, high], coef[0, k, slot, high]], axis=1)
            rows = top.shape[0]
            mixed = jnp.dot(
                jnp.concatenate([top, bottom], axis=0), both, preferred_element_type=jnp.float32
            ).astype(jnp.bfloat16)
            buf[c, low, slot] = mixed[:rows]
            buf[c, high, slot] = mixed[rows:]
            return carry

        lax.fori_loop(0, slots * half, pair, 0)


def kernel(
    n_order, n_level, slot_ref, fourier_ref, self_ref, pair_ref, out_ref,
    cycles, stage, by_cycle, blocks, turned, near, far,
    joined, opened, load_sem, own_sem, z1_sem, xy_sem, z2_sem, z3_sem, coef_sem, core_sem,
):
    o, z, f = lax.axis_index("order"), lax.axis_index("level"), lax.axis_index("freq")
    chunks = stage.shape[0]
    orders, rows, width = stage.shape[2:]
    slots = orders // n_order
    levels = near.shape[1]
    other = 1 - f

    def at_level(d):
        return lax.rem(z + d, n_level)

    def at_order(d):
        return lax.rem(o + d, n_order)

    def loop(count, body):
        lax.fori_loop(1, count, lambda d, carry: (body(d), carry)[1], 0)

    barrier = pltpu.get_barrier_semaphore()

    def greet(d):
        @pl.when(at_level(d) != LEADER)
        def _():
            pl.semaphore_signal(barrier, 1, device_id=(o, at_level(d), f), device_id_type=MESH)

    loop(n_level, greet)
    pl.semaphore_signal(barrier, 1, device_id=(o, z, other), device_id_type=MESH)

    loads = [
        pltpu.make_async_copy(fourier_ref, cycles, load_sem.at[0]),
        pltpu.make_async_copy(self_ref.at[pl.ds(0, levels)], near.at[0], load_sem.at[1]),
        pltpu.make_async_copy(pair_ref.at[pl.ds(0, levels)], near.at[1], load_sem.at[2]),
        pltpu.make_async_copy(self_ref.at[pl.ds(levels, levels), f, z], far.at[0, :, f, z], load_sem.at[3]),
        pltpu.make_async_copy(pair_ref.at[pl.ds(levels, levels), f, z], far.at[1, :, f, z], load_sem.at[4]),
    ]
    for copy in loads:
        copy.start()

    def enter():
        @pl.when(z != LEADER)
        def _():
            pl.semaphore_wait(barrier, n_level)
            pl.semaphore_signal(joined, 1, device_id=(o, LEADER, f), device_id_type=MESH)

        @pl.when(z == LEADER)
        def _():
            pl.semaphore_wait(joined, n_level - 1)

    def herald():
        @pl.when(z == HERALD)
        def _():
            loop(n_order, lambda d: pl.semaphore_signal(
                barrier, 1, device_id=(at_order(d), LEADER, f), device_id_type=MESH
            ))

    def meet_columns():
        @pl.when(z == LEADER)
        def _():
            pl.semaphore_wait(barrier, n_order)
            loop(n_level, lambda d: pl.semaphore_signal(
                opened, 1, device_id=(o, at_level(d), f), device_id_type=MESH
            ))

        @pl.when(z != LEADER)
        def _():
            pl.semaphore_wait(opened, 1)

    def to_level(src, dst, sems, c, d):
        return pltpu.make_async_remote_copy(
            src, dst, sems.at[0, c, d], sems.at[1, c, d],
            device_id=(o, at_level(d), f), device_id_type=MESH,
        )

    def z1(c, d):
        return to_level(stage.at[c, at_level(d)], by_cycle.at[c, z], z1_sem, c, d)

    def xy(c, d):
        return pltpu.make_async_remote_copy(
            by_cycle.at[c, :, pl.ds(at_order(d) * slots, slots)],
            blocks.at[c, :, :, pl.ds(pl.multiple_of(o * rows, rows), rows)],
            xy_sem.at[0, c, d], xy_sem.at[1, c, d],
            device_id=(at_order(d), z, f), device_id_type=MESH,
        )

    def z2(c, d):
        return to_level(blocks.at[c, at_level(d)], turned.at[c, z], z2_sem, c, d)

    def z3(c, d):
        return to_level(
            turned.at[c, at_level(d)], out_ref.at[:, z, :, pl.ds(c * width, width)], z3_sem, c, d
        )

    def coef(which, d):
        src = (self_ref, pair_ref)[which]
        return to_level(
            src.at[pl.ds(levels, levels), f, at_level(d)], far.at[which, :, f, z], coef_sem, which, d
        )

    def core(which):
        return pltpu.make_async_remote_copy(
            far.at[which, :, f], far.at[which, :, f],
            core_sem.at[0, which], core_sem.at[1, which],
            device_id=(o, z, other), device_id_type=MESH,
        )

    own = {}
    for c in range(chunks):
        own["xy", c] = pltpu.make_async_copy(
            by_cycle.at[c, :, pl.ds(o * slots, slots)],
            blocks.at[c, :, :, pl.ds(pl.multiple_of(o * rows, rows), rows)],
            own_sem.at[0, c],
        )
        own["z2", c] = pltpu.make_async_copy(blocks.at[c, z], turned.at[c, z], own_sem.at[1, c])
        own["z3", c] = pltpu.make_async_copy(
            turned.at[c, z], out_ref.at[:, z, :, pl.ds(c * width, width)], own_sem.at[2, c]
        )

    loads[0].wait()
    for c in range(chunks):

        def place(s, carry, c=c):
            order = slot_ref[s]
            stage[c, :, s] = cycles[order, :, :, c * width : (c + 1) * width]
            by_cycle[c, z, s] = cycles[order, z, :, c * width : (c + 1) * width]
            return carry

        lax.fori_loop(0, orders, place, 0)
        if c == 0:
            enter()
        loop(n_level, lambda d: z1(c, d).start())
        if c == 0:
            herald()
    for which in range(2):
        loop(n_level, lambda d: coef(which, d).start())

    for copy in loads[1:]:
        copy.wait()
    for c in range(chunks):
        loop(n_level, lambda d: z1(c, d).wait_recv())
        if c == 0:
            meet_columns()
        loop(n_order, lambda d: xy(c, d).start())
        own["xy", c].start()
        own["xy", c].wait()
        loop(n_order, lambda d: xy(c, d).wait_recv())
        mix(blocks, c, near, levels, slots, n_level)
        loop(n_level, lambda d: z2(c, d).start())
        own["z2", c].start()

    for which in range(2):
        loop(n_level, lambda d: coef(which, d).wait_recv())
        core(which).start()
    for which in range(2):
        core(which).wait_recv()

    for c in range(chunks):
        own["z2", c].wait()
        loop(n_level, lambda d: z2(c, d).wait_recv())
        mix(turned, c, far, levels, slots, n_level)
        loop(n_level, lambda d: z3(c, d).start())
        own["z3", c].start()

    for which in range(2):
        loop(n_level, lambda d: coef(which, d).wait_send())
        core(which).wait_send()
    for c in range(chunks):
        loop(n_level, lambda d: z1(c, d).wait_send())
        loop(n_order, lambda d: xy(c, d).wait_send())
        loop(n_level, lambda d: z2(c, d).wait_send())
        own["z3", c].wait()
        loop(n_level, lambda d: z3(c, d).wait())


def local(n_order, n_level, fourier, order_slot, coeff_self, coeff_pair):
    orders, groups, _, rows, columns = fourier.shape
    all_levels, slots, blocks, cycle_rows, _ = coeff_self.shape
    levels = all_levels // 2
    width = columns // CHUNKS
    dtype = jnp.bfloat16
    hbm = pl.BlockSpec(memory_space=pl.ANY)
    coefs = pltpu.VMEM((2, levels, slots, blocks, cycle_rows, cycle_rows), dtype)
    spread = pltpu.VMEM((CHUNKS, n_level, orders, rows, width), dtype)
    whole = pltpu.VMEM((CHUNKS, n_level, slots, cycle_rows, width), dtype)
    dma = pltpu.SemaphoreType.DMA
    return pl.pallas_call(
        functools.partial(kernel, n_order, n_level),
        out_shape=jax.ShapeDtypeStruct((slots, blocks, cycle_rows, columns), dtype),
        in_specs=[pl.BlockSpec(memory_space=pltpu.SMEM), hbm, hbm, hbm],
        out_specs=hbm,
        scratch_shapes=[
            pltpu.VMEM((orders, groups, rows, columns), dtype),
            spread, spread, whole, whole, coefs, coefs,
            pltpu.SemaphoreType.REGULAR, pltpu.SemaphoreType.REGULAR,
            dma((5,)), dma((3, CHUNKS)),
            dma((2, CHUNKS, n_level)), dma((2, CHUNKS, n_order)),
            dma((2, CHUNKS, n_level)), dma((2, CHUNKS, n_level)),
            dma((2, 2, n_level)), dma((2, 2)),
        ],
        compiler_params=pltpu.CompilerParams(
            collective_id=0, has_side_effects=True, vmem_limit_bytes=50 << 20
        ),
        name="butterfly",
    )(order_slot, fourier.reshape(orders, groups, rows, columns), coeff_self, coeff_pair)


def solution(mesh):
    placed = (
        P("freq", None, "level", "order", None),
        P(),
        P(None, "order", "level", None, None),
        P(None, "order", "level", None, None),
    )
    return jax.shard_map(
        functools.partial(local, mesh.shape["order"], mesh.shape["level"]),
        mesh=mesh,
        in_specs=placed,
        out_specs=P(("freq", "order"), "level", None, None),
        check_vma=False,
    )
```
